32 devices in a mesh: mem: 2 (over y), row: 4 (over x, core), col: 4 (over z).
Axes of the slice: x: 2, y: 2, z: 4, core: 2. Of those that a mesh axis runs over, the one named last changes fastest.
Arguments:
- background_sample: float32 [64, 4, 32, 32, 512], P('mem', None, None, 'row', 'col'), may hold values from -6 to 6
- coupling: float32 [4, 4], replicated, may hold values from -0.6 to 0.6
- diffusion: float32 [32], replicated, may hold values from 0.02 to 0.12
- wind_row: float32 [32], replicated, may hold values from -0.4 to 0.4
- wind_col: float32 [32], replicated, may hold values from -0.4 to 0.4
- observed_entry_index: int32 [64, 32, 512], P(None, 'row', ('col', 'mem')), may hold values from 0 to 127
- obs_value: float32 [64, 32, 512], P(None, 'row', ('col', 'mem')), may hold values from -6 to 6
- obs_weight: float32 [64, 32, 512], P(None, 'row', ('col', 'mem')), may hold values from 0.25 to 4
Outputs:
- analysis: float32 [64, 4, 32, 32, 512], P(None, None, None, 'row', ('col', 'mem'))
The draws below stay inside these ranges and needn't reach their ends.
Inputs may be any that keep to these rules, and one draw needn't show every extreme that they name: observed_entry_index names an entry of a column as variable times 32 plus level.
All inputs are finite; a program needn't handle non-finite values.
Results may differ from the reference program's by a relative error of at most 0.0003.
Values sent between devices are 32-bit elements; how exact they have to be, the bound alone decides.
A program may use at most 256 MiB of HBM per device.

```python
import math
import jax
import jax.numpy as jnp
from jax import lax

MEM = 64
V = 4
L = 32
K = 64
STEPS = 2
NS_ITERS = 2
NR = 32
NC = 512


def place_ends(values, rng, least, largest):
    longest = values.shape.index(max(values.shape))
    spots = []
    for shift in (0, 1):
        where = [jax.random.randint(jax.random.fold_in(rng, axis), (), 0, length) for axis, length in enumerate(values.shape)]
        where[longest] = (where[longest] + shift) % values.shape[longest]
        spots.append(tuple(where))
    return values.at[spots[0]].set(least).at[spots[1]].set(largest)


def block_levels(stream_key, dims, split, smallest, top_value):
    level, own = 1.0, jax.random.fold_in(stream_key, 6)
    for axis_at, shards_of in split:
        heights = jnp.exp(jax.random.uniform(jax.random.fold_in(own, axis_at), (shards_of,), jnp.float32, smallest / len(split), top_value / len(split)))
        level = level * jnp.repeat(heights, dims[axis_at] // shards_of).reshape([-1 if axis == axis_at else 1 for axis in range(len(dims))])
    return level


def gaussian(rng, shape, width, bound, pieces=(), held_as=jnp.bfloat16):
    values = width * jax.random.normal(rng, shape, jnp.float32)
    if pieces:
        values = values * block_levels(rng, shape, pieces, -0.22, 0.18)
    return jnp.clip(values, -bound, bound).astype(held_as)


def setup_inputs(seed: int = 0) -> dict:
    streams_of = jax.random.split(jax.random.key(seed), 9)
    background_sample = gaussian(streams_of[0], (MEM, V, L, NR, NC), 1.0, 6.0, ((0, 2), (3, 4), (4, 4)), jnp.float32)
    coupling = gaussian(streams_of[1], (V, V), 0.15, 0.6, (), jnp.float32)
    diffusion = jnp.clip(jax.random.uniform(streams_of[2], (L,), jnp.float32, 0.02, 0.12), 0.02, 0.12)
    wind_row = jnp.clip(jax.random.uniform(streams_of[3], (L,), jnp.float32, -0.4, 0.4), -0.4, 0.4)
    wind_col = jnp.clip(jax.random.uniform(streams_of[4], (L,), jnp.float32, -0.4, 0.4), -0.4, 0.4)
    observed_entry_index = place_ends(jax.random.randint(streams_of[5], (K, NR, NC), 0, V * L), jax.random.fold_in(streams_of[5], 1), 0, (V * L) - 1).astype(jnp.int32)
    obs_value = gaussian(streams_of[6], (K, NR, NC), 1.0, 6.0, ((1, 4), (2, 8)), jnp.float32)
    obs_weight = jnp.clip(jnp.exp(math.log(4.0) - 2.7725887 * jax.random.uniform(streams_of[7], (K, NR, NC), jnp.float32) ** block_levels(streams_of[7], (K, NR, NC), ((1, 4), (2, 8)), -0.2, 0.2)), 0.25, 4.0)
    return {"background_sample": background_sample, "coupling": coupling, "diffusion": diffusion, "wind_row": wind_row, "wind_col": wind_col, "observed_entry_index": observed_entry_index, "obs_value": obs_value, "obs_weight": obs_weight}


def tendency(padded, diffusion, wind_row, wind_col, coupling):
    centre = padded[..., 1:-1, 1:-1]
    north = padded[..., :-2, 1:-1]
    south = padded[..., 2:, 1:-1]
    west = padded[..., 1:-1, :-2]
    east = padded[..., 1:-1, 2:]
    ensemble_spread = north + south + west + east - 4.0 * centre
    mixed = jnp.einsum('vw,...wlij->...vlij', coupling, centre, precision=lax.Precision.HIGHEST)
    return diffusion[:, None, None] * ensemble_spread - 0.5 * wind_row[:, None, None] * (south - north) - 0.5 * wind_col[:, None, None] * (east - west) + mixed

def bordered(field):
    return jnp.pad(field, ((0, 0), (0, 0), (1, 1), (1, 1)))

def analyse(block, index, value, weight):
    members = block.shape[0]
    entries = block.shape[1]
    highest = lax.Precision.HIGHEST
    mean = lax.optimization_barrier(jnp.mean(block, axis=0))
    pert = block - mean[None]
    onehot = (index[:, None, :] == jnp.arange(entries, dtype=jnp.int32)[None, :, None]).astype(jnp.float32)
    measurement_data = jnp.einsum('mvc,kvc->mkc', block, onehot, precision=highest)
    obs_mean = lax.optimization_barrier(jnp.mean(measurement_data, axis=0))
    obs_pert = measurement_data - obs_mean[None]
    scaled = obs_pert * weight[None]
    eye = jnp.eye(members, dtype=jnp.float32)[:, :, None]
    system = jnp.einsum('mkc,nkc->mnc', scaled, obs_pert, precision=highest) + (members - 1.0) * eye
    scale = jnp.sqrt(lax.optimization_barrier(jnp.sum(system * system, axis=(0, 1))))
    current = system / scale[None, None]
    inverse = jnp.broadcast_to(eye, system.shape)
    for sweep in range(NS_ITERS):
        factor = 1.5 * eye - 0.5 * jnp.einsum('mjc,jnc->mnc', inverse, current, precision=highest)
        current = jnp.einsum('mjc,jnc->mnc', current, factor, precision=highest)
        inverse = jnp.einsum('mjc,jnc->mnc', factor, inverse, precision=highest)
    gain_vec = jnp.einsum('mkc,kc->mc', scaled, value - obs_mean, precision=highest)
    half_vec = jnp.einsum('mjc,jc->mc', inverse, gain_vec, precision=highest)
    centre = jnp.einsum('mjc,jc->mc', inverse, half_vec, precision=highest) / scale[None]
    analysis_coefficients = inverse * jnp.sqrt((members - 1.0) / scale)[None, None] + centre[:, None, :]
    return mean[None] + jnp.einsum('mvc,mnc->nvc', pert, analysis_coefficients, precision=highest)

def reference(background_sample, coupling, diffusion, wind_row, wind_col, observed_entry_index, obs_value, obs_weight):

    def background_prediction(sample_number):
        state = sample_number
        for step in range(STEPS):
            first = tendency(bordered(state), diffusion, wind_row, wind_col, coupling)
            middle = state + first
            second = tendency(bordered(middle), diffusion, wind_row, wind_col, coupling)
            state = state + 0.5 * (first + second)
        return state
    sample_fields = lax.map(background_prediction, background_sample)
    members = sample_fields.shape[0]
    flat = sample_fields.reshape(members, V * L, NR, NC)

    def per_row(row_number):
        block = lax.dynamic_index_in_dim(flat, row_number, 2, keepdims=False)
        index = lax.dynamic_index_in_dim(observed_entry_index, row_number, 1, keepdims=False)
        value = lax.dynamic_index_in_dim(obs_value, row_number, 1, keepdims=False)
        weight = lax.dynamic_index_in_dim(obs_weight, row_number, 1, keepdims=False)
        return analyse(block, index, value, weight)
    result = lax.map(per_row, jnp.arange(NR, dtype=jnp.int32))
    return jnp.moveaxis(result, 0, 2).reshape(members, V, L, NR, NC)
```

```python
import jax
import jax.numpy as jnp
from jax import lax
from jax.experimental import pallas as pl
from jax.experimental.pallas import tpu as pltpu
from jax.sharding import PartitionSpec as P

STEPS = 2


def extended(value, sides, width):
    for axis, dim in sides:
        count, length = (lax.axis_size(axis), value.shape[dim])
        up = [(i, (i + 1) % count) for i in range(count - 1)]
        down = [(j, i) for i, j in up]
        last = lax.slice_in_dim(value, length - width, length, axis=dim)
        first = lax.slice_in_dim(value, 0, width, axis=dim)
        before = lax.ppermute(last, axis, up)
        after = lax.ppermute(first, axis, down)
        value = jnp.concatenate([before, value, after], axis=dim)
    return value


def tendency(padded, diffusion, wind_row, wind_col, coupling):
    centre = padded[..., 1:-1, 1:-1]
    north = padded[..., :-2, 1:-1]
    south = padded[..., 2:, 1:-1]
    west = padded[..., 1:-1, :-2]
    east = padded[..., 1:-1, 2:]
    ensemble_spread = north + south + west + east - 4.0 * centre
    mixed = jnp.einsum("vw,...wlij->...vlij", coupling, centre, precision=lax.Precision.HIGHEST)
    return (
        diffusion[:, None, None] * ensemble_spread
        - 0.5 * wind_row[:, None, None] * (south - north)
        - 0.5 * wind_col[:, None, None] * (east - west)
        + mixed
    )


def rimmed(field):
    return extended(field, (("row", 3), ("col", 4)), 1)


def begin(state):
    return (state, 0)


def propagate_model(state, margin_width, diffusion, wind_row, wind_col, coupling):
    first = tendency(rimmed(state), diffusion, wind_row, wind_col, coupling)
    middle = state + first
    second = tendency(rimmed(middle), diffusion, wind_row, wind_col, coupling)
    return (state + 0.5 * (first + second), margin_width)


def split(value):
    high = value.astype(jnp.bfloat16)
    return high, (value - high.astype(jnp.float32)).astype(jnp.bfloat16)


def doubled(high, low, left):
    both = jnp.where(left, high.astype(jnp.float32), low.astype(jnp.float32)).astype(jnp.bfloat16)
    return jnp.concatenate([both, both], axis=1)


def stacked(high, low):
    return jnp.concatenate([high, high, low, low], axis=0)


def product(left, right):
    return lax.dot_general(left, right, (((1,), (0,)), ((), ())), preferred_element_type=jnp.float32)


def product_t(left, right):
    return lax.dot_general(left, right, (((1,), (1,)), ((), ())), preferred_element_type=jnp.float32)


def analysis_kernel(x_ref, index_ref, root_ref, value_ref, out_ref):
    count, members, entries = x_ref.shape
    cells = range(count)
    lane = lax.broadcasted_iota(jnp.int32, (members, 2 * members), 1)
    row = lax.broadcasted_iota(jnp.int32, (members, 2 * members), 0)
    left = lane < members
    left_tall = lax.broadcasted_iota(jnp.int32, (members + 16, 2 * members), 1) < members
    eye = jnp.where((lane == row) | (lane == row + members), 1.0, 0.0).astype(jnp.float32)
    means, perts, systems, gains = [], [], [], []
    for b in cells:
        x = x_ref[b]
        mean = jnp.sum(x, axis=0, keepdims=True) * (1.0 / members)
        pert = x - mean
        index = jnp.broadcast_to(index_ref[b : b + 1], (members, entries))
        observed = jnp.take_along_axis(pert, index, axis=1)
        obs_mean = jnp.take_along_axis(jnp.broadcast_to(mean, (8, entries)), index[:8], axis=1)
        root = root_ref[b : b + 1]
        innovation = (value_ref[b : b + 1] - obs_mean) * root
        scaled = observed * root
        high, low = split(jnp.concatenate([scaled, innovation, innovation], axis=0))
        ahigh, alow = high[:members], low[:members]
        wide = jnp.concatenate(
            [jnp.concatenate([ahigh, alow], axis=1), jnp.concatenate([ahigh, alow], axis=1)], axis=0
        )
        both = product_t(doubled(high, low, left_tall), wide)
        means.append(mean)
        perts.append(pert)
        systems.append(both[:members] + (members - 1.0) * eye)
        gains.append(both[members : members + 1])
    inverses, rates = [], []
    for b in cells:
        total = 0.5 * jnp.sum(jnp.sum(systems[b] * systems[b], axis=0, keepdims=True), axis=1, keepdims=True)
        rates.append(lax.rsqrt(total))
    for b in cells:
        current = systems[b] * rates[b]
        high, low = split(current)
        square = product(doubled(high, low, left), stacked(high, low))
        shigh, slow = split(square)
        high, low = split(0.0625 * square - 0.5625 * current)
        rest = product(doubled(shigh, slow, left), stacked(high, low))
        inverses.append(2.25 * eye - 2.4375 * current + 1.6875 * square + rest)
    for b in cells:
        high, low = split(inverses[b])
        phigh, plow = split(perts[b])
        moved = product(doubled(high, low, left), stacked(phigh, plow))
        half = 0.5 * jnp.sum(inverses[b] * gains[b], axis=1, keepdims=True)
        shift = jnp.sum(moved * half, axis=0, keepdims=True) * rates[b]
        out_ref[b] = moved * jnp.sqrt((members - 1.0) * rates[b]) + (means[b] + shift)


def analyse(flat, index, value, weight):
    cells, members, entries = flat.shape
    count = 8
    small = pl.BlockSpec((count, index.shape[1]), lambda i: (i, 0))
    large = pl.BlockSpec((count, members, entries), lambda i: (i, 0, 0))
    return pl.pallas_call(
        analysis_kernel,
        grid=(cells // count,),
        in_specs=[large, small, small, small],
        out_specs=large,
        out_shape=jax.ShapeDtypeStruct(flat.shape, flat.dtype),
    )(flat, index, jnp.sqrt(weight), value)


def body(
    background_sample,
    coupling,
    diffusion,
    wind_row,
    wind_col,
    observed_entry_index,
    obs_value,
    obs_weight,
):
    state, margin_width = begin(background_sample)
    for step in range(STEPS):
        state, margin_width = propagate_model(
            state, margin_width, diffusion, wind_row, wind_col, coupling
        )
    moved = lax.all_to_all(state, "mem", split_axis=4, concat_axis=0, tiled=True)
    members, variables, levels, rows_local, cols_local = moved.shape
    cells = rows_local * cols_local
    flat = moved.reshape(members, variables * levels, cells).transpose(2, 0, 1)

    def listed(array):
        array = array.reshape(array.shape[0], cells).T
        return jnp.concatenate([array, array], axis=1)

    result = analyse(flat, listed(observed_entry_index), listed(obs_value), listed(obs_weight))
    result = result.transpose(1, 2, 0)
    return result.reshape(members, variables, levels, rows_local, cols_local)


def solution(mesh):
    placed = (
        P("mem", None, None, "row", "col"),
        P(),
        P(),
        P(),
        P(),
        P(None, "row", ("col", "mem")),
        P(None, "row", ("col", "mem")),
        P(None, "row", ("col", "mem")),
    )
    return jax.shard_map(
        body,
        mesh=mesh,
        in_specs=placed,
        out_specs=P(None, None, None, "row", ("col", "mem")),
        check_vma=False,
    )
```

```python
import jax
import jax.numpy as jnp
from jax import lax
from jax.experimental import pallas as pl
from jax.experimental.pallas import tpu as pltpu
from jax.sharding import PartitionSpec as P

STEPS = 2
PARTS = 2


def pack(value, place, lane, sides):
    west, east = sides
    here = lane == place
    return (
        jnp.where(here, pltpu.roll(value, place, 1), west),
        jnp.where(here, pltpu.roll(value, place + 1, 1), east),
    )


def borders_kernel(x_ref, north_ref, south_ref, west_ref, east_ref):
    _, variables, levels, rows, cols = x_ref.shape
    lane = lax.broadcasted_iota(jnp.int32, (rows, cols), 1)

    def level(l, sides):
        for v in range(variables):
            value, place = x_ref[0, v, l], v * levels + l
            north_ref[0, pl.ds(place, 1), :] = value[:1]
            south_ref[0, pl.ds(place, 1), :] = value[rows - 1 :]
            sides = pack(value, place, lane, sides)
        return sides

    zero = jnp.zeros((rows, cols), jnp.float32)
    west_ref[0], east_ref[0] = lax.fori_loop(0, levels, level, (zero, zero), unroll=2)


def advance_kernel(final, paired, level_ref, mix_ref, *refs):
    x_ref, refs = refs[0], refs[1:]
    base_ref = None
    if paired:
        base_ref, refs = refs[0], refs[1:]
    north_ref, south_ref, west_ref, east_ref, out_ref = refs[:5]
    refs = refs[5:]
    _, variables, levels, rows, cols = x_ref.shape
    lane = lax.broadcasted_iota(jnp.int32, (rows, cols), 1)
    row = lax.broadcasted_iota(jnp.int32, (rows, cols), 0)
    west_halo, east_halo = west_ref[0], east_ref[0]

    def level(l, sides):
        values = [x_ref[0, v, l] for v in range(variables)]
        north_c, south_c, west_c, east_c, centre_c = [level_ref[i, l] for i in range(5)]
        for v in range(variables):
            value, place = values[v], v * levels + l
            north = jnp.where(row == 0, north_ref[0, pl.ds(place, 1), :], pltpu.roll(value, 1, 0))
            south = jnp.where(
                row == rows - 1, south_ref[0, pl.ds(place, 1), :], pltpu.roll(value, rows - 1, 0)
            )
            west = jnp.where(lane == 0, pltpu.roll(west_halo, cols - place, 1), pltpu.roll(value, 1, 1))
            east = jnp.where(
                lane == cols - 1, pltpu.roll(east_halo, cols - 1 - place, 1), pltpu.roll(value, cols - 1, 1)
            )
            change = north_c * north + south_c * south + west_c * west + east_c * east
            change = change + (centre_c + mix_ref[v, v]) * value
            for w in range(variables):
                if w != v:
                    change = change + mix_ref[v, w] * values[w]
            result = value + change
            if paired:
                result = 0.5 * (base_ref[0, v, l] + result)
            if final:
                scratch = refs[0]
                scratch[pl.ds(pl.multiple_of(place * rows, rows), rows), :] = result
            else:
                out_ref[0, v, l] = result
                refs[0][0, pl.ds(place, 1), :] = result[:1]
                refs[1][0, pl.ds(place, 1), :] = result[rows - 1 :]
                sides = pack(result, place, lane, sides)
        return sides

    zero = jnp.zeros((rows, cols), jnp.float32)
    sides = lax.fori_loop(0, levels, level, (zero, zero), unroll=2)
    if not final:
        refs[2][0], refs[3][0] = sides
        return
    groups, width = out_ref.shape[0], out_ref.shape[3]
    for r in range(rows):
        turned = refs[0][pl.ds(r, variables * levels, stride=rows), :].T
        for g in range(groups):
            out_ref[g, 0, r] = turned[g * width : (g + 1) * width]


def edge_specs(shape):
    members, variables, levels, rows, cols = shape
    line = (members, variables * levels, cols)
    side = (members, rows, cols)
    shapes = [jax.ShapeDtypeStruct(d, jnp.float32) for d in (line, line, side, side)]
    specs = [pl.BlockSpec((1,) + d.shape[1:], lambda i: (i, 0, 0)) for d in shapes]
    return shapes, specs


def borders(x):
    shapes, specs = edge_specs(x.shape)
    return pl.pallas_call(
        borders_kernel,
        grid=(x.shape[0],),
        in_specs=[pl.BlockSpec((1,) + x.shape[1:], lambda i: (i, 0, 0, 0, 0))],
        out_specs=specs,
        out_shape=shapes,
        cost_estimate=pl.CostEstimate(flops=x.size * 4, bytes_accessed=x.size * 4, transcendentals=0),
    )(x)


def exchanged(edges):
    north, south, west, east = edges

    def shifted(value, axis, step):
        count = lax.axis_size(axis)
        pairs = [(i, i + 1) for i in range(count - 1)]
        return lax.ppermute(value, axis, pairs if step > 0 else [(j, i) for i, j in pairs])

    return [
        shifted(south, "row", 1),
        shifted(north, "row", -1),
        shifted(east, "col", 1),
        shifted(west, "col", -1),
    ]


def advance(x, base, halos, by_level, mix, final):
    members, variables, levels, rows, cols = x.shape
    shapes, specs = edge_specs(x.shape)
    block = pl.BlockSpec((1,) + x.shape[1:], lambda i: (i, 0, 0, 0, 0))
    scalars = pl.BlockSpec(memory_space=pltpu.SMEM)
    fields = [x] if base is None else [x, base]
    scratch = []
    if final:
        groups = lax.axis_size("mem")
        turned = (groups, members, rows, cols // groups, variables * levels)
        out_shape = [jax.ShapeDtypeStruct(turned, jnp.float32)]
        out_specs = [
            pl.BlockSpec((groups, 1) + turned[2:], lambda i: (0, i, 0, 0, 0))
        ]
        scratch = [pltpu.VMEM((variables * levels * rows, cols), jnp.float32)]
    else:
        out_shape = [jax.ShapeDtypeStruct(x.shape, jnp.float32)] + shapes
        out_specs = [block] + specs
    out = pl.pallas_call(
        lambda *refs: advance_kernel(final, base is not None, *refs),
        grid=(members,),
        in_specs=[scalars, scalars] + [block] * len(fields) + specs,
        out_specs=out_specs,
        out_shape=out_shape,
        scratch_shapes=scratch,
        cost_estimate=pl.CostEstimate(flops=x.size * 40, bytes_accessed=x.size * 12, transcendentals=0),
    )(by_level, mix, *fields, *halos)
    return out[0], out[1:]


def split(value):
    high = value.astype(jnp.bfloat16)
    return high, (value - high.astype(jnp.float32)).astype(jnp.bfloat16)


def doubled(high, low, left):
    both = jnp.where(left, high.astype(jnp.float32), low.astype(jnp.float32)).astype(jnp.bfloat16)
    return jnp.concatenate([both, both], axis=1)


def stacked(high, low):
    return jnp.concatenate([high, high, low, low], axis=0)


def product(left, right):
    return lax.dot_general(left, right, (((1,), (0,)), ((), ())), preferred_element_type=jnp.float32)


def product_t(left, right):
    return lax.dot_general(left, right, (((1,), (1,)), ((), ())), preferred_element_type=jnp.float32)


def analysis_kernel(first_ref, second_ref, index_ref, root_ref, value_ref, out_ref):
    sources, part, count, entries = first_ref.shape
    members = 2 * sources * part
    halves = [ref.reshape(sources * part * count, entries) for ref in (first_ref, second_ref)]
    cells = range(count)
    lane = lax.broadcasted_iota(jnp.int32, (members, 2 * members), 1)
    row = lax.broadcasted_iota(jnp.int32, (members, 2 * members), 0)
    left = lane < members
    left_tall = lax.broadcasted_iota(jnp.int32, (members + 16, 2 * members), 1) < members
    eye = jnp.where((lane == row) | (lane == row + members), 1.0, 0.0).astype(jnp.float32)
    means, perts, systems, gains = [], [], [], []
    for b in cells:
        x = jnp.concatenate([ref[pl.ds(b, sources * part, stride=count), :] for ref in halves], axis=0)
        mean = jnp.sum(x, axis=0, keepdims=True) * (1.0 / members)
        pert = x - mean
        index = jnp.broadcast_to(index_ref[b : b + 1], (members, entries))
        observed = jnp.take_along_axis(pert, index, axis=1)
        obs_mean = jnp.take_along_axis(jnp.broadcast_to(mean, (8, entries)), index[:8], axis=1)
        root = root_ref[b : b + 1]
        innovation = (value_ref[b : b + 1] - obs_mean) * root
        scaled = observed * root
        high, low = split(jnp.concatenate([scaled, innovation, innovation], axis=0))
        ahigh, alow = high[:members], low[:members]
        wide = jnp.concatenate(
            [jnp.concatenate([ahigh, alow], axis=1), jnp.concatenate([ahigh, alow], axis=1)], axis=0
        )
        both = product_t(doubled(high, low, left_tall), wide)
        means.append(mean)
        perts.append(pert)
        systems.append(both[:members] + (members - 1.0) * eye)
        gains.append(both[members : members + 1])
    inverses, rates = [], []
    for b in cells:
        total = 0.5 * jnp.sum(jnp.sum(systems[b] * systems[b], axis=0, keepdims=True), axis=1, keepdims=True)
        rates.append(lax.rsqrt(total))
    for b in cells:
        current = systems[b] * rates[b]
        high, low = split(current)
        square = product(doubled(high, low, left), stacked(high, low))
        shigh, slow = split(square)
        high, low = split(0.0625 * square - 0.5625 * current)
        rest = product(doubled(shigh, slow, left), stacked(high, low))
        inverses.append(2.25 * eye - 2.4375 * current + 1.6875 * square + rest)
    for b in cells:
        high, low = split(inverses[b])
        phigh, plow = split(perts[b])
        moved = product(doubled(high, low, left), stacked(phigh, plow))
        half = 0.5 * jnp.sum(inverses[b] * gains[b], axis=1, keepdims=True)
        shift = jnp.sum(moved * half, axis=0, keepdims=True) * rates[b]
        result = moved * jnp.sqrt((members - 1.0) * rates[b]) + (means[b] + shift)
        for half in range(2):
            for source in range(sources):
                start, at = (half * sources + source) * part, (2 * source + half) * part
                out_ref[b, at : at + part, :] = result[start : start + part]


def analyse(halves, index, value, weight):
    sources, part, cells, entries = halves[0].shape
    members = 2 * sources * part
    count = 8
    small = pl.BlockSpec((count, index.shape[1]), lambda i: (i, 0))
    large = pl.BlockSpec((count, members, entries), lambda i: (i, 0, 0))
    half = pl.BlockSpec((sources, part, count, entries), lambda i: (0, 0, i, 0))
    return pl.pallas_call(
        analysis_kernel,
        grid=(cells // count,),
        in_specs=[half, half, small, small, small],
        out_specs=large,
        out_shape=jax.ShapeDtypeStruct((cells, members, entries), jnp.float32),
    )(*halves, index, jnp.sqrt(weight), value)


def body(
    background_sample,
    coupling,
    diffusion,
    wind_row,
    wind_col,
    observed_entry_index,
    obs_value,
    obs_weight,
):
    members, variables, levels, rows, cols = background_sample.shape
    by_level = jnp.stack(
        [
            diffusion + 0.5 * wind_row,
            diffusion - 0.5 * wind_row,
            diffusion + 0.5 * wind_col,
            diffusion - 0.5 * wind_col,
            -4.0 * diffusion,
        ]
    )
    part = members // PARTS
    states = [background_sample[i * part : (i + 1) * part] for i in range(PARTS)]
    edges = [borders(state) for state in states]
    middles = [None] * PARTS
    for step in range(STEPS):
        last = step == STEPS - 1
        for i in range(PARTS):
            middles[i], edges[i] = advance(
                states[i], None, exchanged(edges[i]), by_level, coupling, False
            )
        for i in range(PARTS):
            states[i], edges[i] = advance(
                middles[i], states[i], exchanged(edges[i]), by_level, coupling, last
            )
    sources = lax.axis_size("mem")
    cells = rows * (cols // sources)
    halves = [
        lax.all_to_all(state, "mem", split_axis=0, concat_axis=0).reshape(
            sources, part, cells, variables * levels
        )
        for state in states
    ]

    def listed(array):
        array = array.reshape(array.shape[0], cells).T
        return jnp.concatenate([array, array], axis=1)

    result = analyse(halves, listed(observed_entry_index), listed(obs_value), listed(obs_weight))
    result = result.transpose(1, 2, 0)
    return result.reshape(result.shape[0], variables, levels, rows, cols // sources)


def solution(mesh):
    placed = (
        P("mem", None, None, "row", "col"),
        P(),
        P(),
        P(),
        P(),
        P(None, "row", ("col", "mem")),
        P(None, "row", ("col", "mem")),
        P(None, "row", ("col", "mem")),
    )
    return jax.shard_map(
        body,
        mesh=mesh,
        in_specs=placed,
        out_specs=P(None, None, None, "row", ("col", "mem")),
        check_vma=False,
    )
```

```python
import jax
import jax.numpy as jnp
from jax import lax
from jax.experimental import pallas as pl
from jax.experimental.pallas import tpu as pltpu
from jax.sharding import PartitionSpec as P

STEPS = 2
PARTS = 2
ORDER = ((0, 0), (1, 0), (0, 1), (1, 1), (0, 2), (0, 3), (1, 2), (1, 3))


def pack(value, place, lane, sides):
    west, east = sides
    here = lane == place
    return (
        jnp.where(here, pltpu.roll(value, place, 1), west),
        jnp.where(here, pltpu.roll(value, place + 1, 1), east),
    )


def borders_kernel(x_ref, north_ref, south_ref, west_ref, east_ref):
    _, variables, levels, rows, cols = x_ref.shape
    lane = lax.broadcasted_iota(jnp.int32, (rows, cols), 1)

    def level(l, sides):
        for v in range(variables):
            value, place = x_ref[0, v, l], v * levels + l
            north_ref[0, pl.ds(place, 1), :] = value[:1]
            south_ref[0, pl.ds(place, 1), :] = value[rows - 1 :]
            sides = pack(value, place, lane, sides)
        return sides

    zero = jnp.zeros((rows, cols), jnp.float32)
    west_ref[0], east_ref[0] = lax.fori_loop(0, levels, level, (zero, zero), unroll=8)


def advance_kernel(final, paired, level_ref, mix_ref, *refs):
    x_ref, refs = refs[0], refs[1:]
    base_ref = None
    if paired:
        base_ref, refs = refs[0], refs[1:]
    north_ref, south_ref, west_ref, east_ref, out_ref = refs[:5]
    refs = refs[5:]
    _, variables, levels, rows, cols = x_ref.shape
    lane = lax.broadcasted_iota(jnp.int32, (rows, cols), 1)
    row = lax.broadcasted_iota(jnp.int32, (rows, cols), 0)
    west_halo, east_halo = west_ref[0], east_ref[0]

    def level(l, sides):
        values = [x_ref[0, v, l] for v in range(variables)]
        north_c, south_c, west_c, east_c, centre_c = [level_ref[i, l] for i in range(5)]
        for v in range(variables):
            value, place = values[v], v * levels + l
            north = jnp.where(row == 0, north_ref[0, pl.ds(place, 1), :], pltpu.roll(value, 1, 0))
            south = jnp.where(
                row == rows - 1, south_ref[0, pl.ds(place, 1), :], pltpu.roll(value, rows - 1, 0)
            )
            west = jnp.where(lane == 0, pltpu.roll(west_halo, cols - place, 1), pltpu.roll(value, 1, 1))
            east = jnp.where(
                lane == cols - 1, pltpu.roll(east_halo, cols - 1 - place, 1), pltpu.roll(value, cols - 1, 1)
            )
            change = north_c * north + south_c * south + west_c * west + east_c * east
            change = change + (centre_c + mix_ref[v, v]) * value
            for w in range(variables):
                if w != v:
                    change = change + mix_ref[v, w] * values[w]
            result = value + change
            if paired:
                result = 0.5 * (base_ref[0, v, l] + result)
            if final:
                scratch = refs[0]
                scratch[pl.ds(pl.multiple_of(place * rows, rows), rows), :] = result
            else:
                out_ref[0, v, l] = result
                refs[0][0, pl.ds(place, 1), :] = result[:1]
                refs[1][0, pl.ds(place, 1), :] = result[rows - 1 :]
                sides = pack(result, place, lane, sides)
        return sides

    zero = jnp.zeros((rows, cols), jnp.float32)
    sides = lax.fori_loop(0, levels, level, (zero, zero), unroll=8)
    if not final:
        refs[2][0], refs[3][0] = sides
        return
    groups, width = out_ref.shape[0], out_ref.shape[3]
    for r in range(rows):
        turned = refs[0][pl.ds(r, variables * levels, stride=rows), :].T
        for g in range(groups):
            out_ref[g, 0, r] = turned[g * width : (g + 1) * width]


def edge_specs(shape):
    members, variables, levels, rows, cols = shape
    line = (members, variables * levels, cols)
    side = (members, rows, cols)
    shapes = [jax.ShapeDtypeStruct(d, jnp.float32) for d in (line, line, side, side)]
    specs = [pl.BlockSpec((1,) + d.shape[1:], lambda i: (i, 0, 0)) for d in shapes]
    return shapes, specs


def member_spec(x, start):
    return pl.BlockSpec((1,) + x.shape[1:], lambda i: (i + start, 0, 0, 0, 0))


def borders(state, part):
    x, start = state
    shapes, specs = edge_specs((part,) + x.shape[1:])
    return pl.pallas_call(
        borders_kernel,
        grid=(part,),
        in_specs=[member_spec(x, start)],
        out_specs=specs,
        out_shape=shapes,
        cost_estimate=pl.CostEstimate(flops=x.size, bytes_accessed=x.size * 4, transcendentals=0),
    )(x)


def exchanged(edges):
    north, south, west, east = edges

    def shifted(value, axis, step):
        count = lax.axis_size(axis)
        pairs = [(i, i + 1) for i in range(count - 1)]
        return lax.ppermute(value, axis, pairs if step > 0 else [(j, i) for i, j in pairs])

    return [
        shifted(south, "row", 1),
        shifted(north, "row", -1),
        shifted(east, "col", 1),
        shifted(west, "col", -1),
    ]


def advance(state, base, halos, by_level, mix, final):
    members, (_, variables, levels, rows, cols) = halos[0].shape[0], state[0].shape
    shape = (members, variables, levels, rows, cols)
    size = members * variables * levels * rows * cols
    shapes, specs = edge_specs(shape)
    scalars = pl.BlockSpec(memory_space=pltpu.SMEM)
    fields = [state] if base is None else [state, base]
    scratch = []
    if final:
        groups = lax.axis_size("mem")
        turned = (groups, members, rows, cols // groups, variables * levels)
        out_shape = [jax.ShapeDtypeStruct(turned, jnp.float32)]
        out_specs = [
            pl.BlockSpec((groups, 1) + turned[2:], lambda i: (0, i, 0, 0, 0))
        ]
        scratch = [pltpu.VMEM((variables * levels * rows, cols), jnp.float32)]
    else:
        out_shape = [jax.ShapeDtypeStruct(shape, jnp.float32)] + shapes
        out_specs = [pl.BlockSpec((1,) + shape[1:], lambda i: (i, 0, 0, 0, 0))] + specs
    out = pl.pallas_call(
        lambda *refs: advance_kernel(final, base is not None, *refs),
        grid=(members,),
        in_specs=[scalars, scalars] + [member_spec(*field) for field in fields] + specs,
        out_specs=out_specs,
        out_shape=out_shape,
        scratch_shapes=scratch,
        cost_estimate=pl.CostEstimate(flops=size * 40, bytes_accessed=size * 48, transcendentals=0),
    )(by_level, mix, *[field[0] for field in fields], *halos)
    return (out[0], 0), out[1:]


def split(value):
    high = value.astype(jnp.bfloat16)
    return high, (value - high.astype(jnp.float32)).astype(jnp.bfloat16)


def doubled(high, low, left):
    both = jnp.where(left, high.astype(jnp.float32), low.astype(jnp.float32)).astype(jnp.bfloat16)
    return jnp.concatenate([both, both], axis=1)


def stacked(high, low):
    return jnp.concatenate([high, high, low, low], axis=0)


def product(left, right):
    return lax.dot_general(left, right, (((1,), (0,)), ((), ())), preferred_element_type=jnp.float32)


def product_t(left, right):
    return lax.dot_general(left, right, (((1,), (1,)), ((), ())), preferred_element_type=jnp.float32)


def analysis_kernel(first_ref, second_ref, index_ref, root_ref, value_ref, out_ref):
    sources, part, count, entries = first_ref.shape
    members = 2 * sources * part
    halves = [ref.reshape(sources * part * count, entries) for ref in (first_ref, second_ref)]
    placed = out_ref.reshape(members * count, entries)
    cells = range(count)
    lane = lax.broadcasted_iota(jnp.int32, (members, 2 * members), 1)
    row = lax.broadcasted_iota(jnp.int32, (members, 2 * members), 0)
    left = lane < members
    left_tall = lax.broadcasted_iota(jnp.int32, (members + 16, 2 * members), 1) < members
    eye = jnp.where((lane == row) | (lane == row + members), 1.0, 0.0).astype(jnp.float32)
    means, perts, systems, gains = [], [], [], []
    for b in cells:
        x = jnp.concatenate([ref[pl.ds(b, sources * part, stride=count), :] for ref in halves], axis=0)
        mean = jnp.sum(x, axis=0, keepdims=True) * (1.0 / members)
        pert = x - mean
        index = jnp.broadcast_to(index_ref[b : b + 1], (members, entries))
        observed = jnp.take_along_axis(pert, index, axis=1)
        obs_mean = jnp.take_along_axis(jnp.broadcast_to(mean, (8, entries)), index[:8], axis=1)
        root = root_ref[b : b + 1]
        innovation = (value_ref[b : b + 1] - obs_mean) * root
        scaled = observed * root
        high, low = split(jnp.concatenate([scaled, innovation, innovation], axis=0))
        ahigh, alow = high[:members], low[:members]
        wide = jnp.concatenate(
            [jnp.concatenate([ahigh, alow], axis=1), jnp.concatenate([ahigh, alow], axis=1)], axis=0
        )
        both = product_t(doubled(high, low, left_tall), wide)
        means.append(mean)
        perts.append(pert)
        systems.append(both[:members] + (members - 1.0) * eye)
        gains.append(both[members : members + 1])
    inverses, rates = [], []
    for b in cells:
        total = 0.5 * jnp.sum(jnp.sum(systems[b] * systems[b], axis=0, keepdims=True), axis=1, keepdims=True)
        rates.append(lax.rsqrt(total))
    for b in cells:
        current = systems[b] * rates[b]
        high, low = split(current)
        square = product(doubled(high, low, left), stacked(high, low))
        shigh, slow = split(square)
        high, low = split(0.0625 * square - 0.5625 * current)
        rest = product(doubled(shigh, slow, left), stacked(high, low))
        inverses.append(2.25 * eye - 2.4375 * current + 1.6875 * square + rest)
    for b in cells:
        high, low = split(inverses[b])
        phigh, plow = split(perts[b])
        moved = product(doubled(high, low, left), stacked(phigh, plow))
        half = 0.5 * jnp.sum(inverses[b] * gains[b], axis=1, keepdims=True)
        shift = jnp.sum(moved * half, axis=0, keepdims=True) * rates[b]
        result = moved * jnp.sqrt((members - 1.0) * rates[b]) + (means[b] + shift)
        for half in range(2):
            for source in range(sources):
                start, at = (half * sources + source) * part, (2 * source + half) * part
                placed[pl.ds(at * count + b, part, stride=count), :] = result[start : start + part]


def analyse(halves, index, value, weight):
    sources, part, cells, entries = halves[0].shape
    members = 2 * sources * part
    count = 8
    small = pl.BlockSpec((count, index.shape[1]), lambda i: (i, 0))
    large = pl.BlockSpec((members, count, entries), lambda i: (0, i, 0))
    half = pl.BlockSpec((sources, part, count, entries), lambda i: (0, 0, i, 0))
    return pl.pallas_call(
        analysis_kernel,
        grid=(cells // count,),
        in_specs=[half, half, small, small, small],
        out_specs=large,
        out_shape=jax.ShapeDtypeStruct((members, cells, entries), jnp.float32),
    )(*halves, index, jnp.sqrt(weight), value)


def spread_kernel(x_ref, out_ref):
    _, cells, entries = x_ref.shape
    rows = out_ref.shape[1] // entries
    width = cells // rows
    placed = out_ref.at[0]
    turned = x_ref[0].T
    for r in range(rows):
        placed[pl.ds(r, entries, stride=rows), :] = turned[:, r * width : (r + 1) * width]


def spread(x, rows):
    members, cells, entries = x.shape
    shape = (members, entries * rows, cells // rows)
    return pl.pallas_call(
        spread_kernel,
        grid=(members,),
        in_specs=[pl.BlockSpec((1, cells, entries), lambda i: (i, 0, 0))],
        out_specs=pl.BlockSpec((1,) + shape[1:], lambda i: (i, 0, 0)),
        out_shape=jax.ShapeDtypeStruct(shape, jnp.float32),
    )(x)


def body(
    background_sample,
    coupling,
    diffusion,
    wind_row,
    wind_col,
    observed_entry_index,
    obs_value,
    obs_weight,
):
    members, variables, levels, rows, cols = background_sample.shape
    by_level = jnp.stack(
        [
            diffusion + 0.5 * wind_row,
            diffusion - 0.5 * wind_row,
            diffusion + 0.5 * wind_col,
            diffusion - 0.5 * wind_col,
            -4.0 * diffusion,
        ]
    )
    part = members // PARTS
    states = [(background_sample, i * part) for i in range(PARTS)]
    edges = [borders(state, part) for state in states]
    halos = [exchanged(edge) for edge in edges]
    middles = [None] * PARTS
    gate = None
    for i, turn in ORDER:
        table = by_level if gate is None else lax.optimization_barrier((by_level, gate))[0]
        if turn % 2 == 0:
            middles[i], edge = advance(states[i], None, halos[i], table, coupling, False)
        else:
            last = turn == 2 * STEPS - 1
            states[i], edge = advance(middles[i], states[i], halos[i], table, coupling, last)
        if edge:
            gate, halos[i] = edge[2], exchanged(edge)
        else:
            gate = states[i][0][:1, :1, :1, :1, :1]
    sources = lax.axis_size("mem")
    cells = rows * (cols // sources)
    halves = [
        lax.all_to_all(state, "mem", split_axis=0, concat_axis=0).reshape(
            sources, part, cells, variables * levels
        )
        for state, _ in states
    ]

    def listed(array):
        array = array.reshape(array.shape[0], cells).T
        return jnp.concatenate([array, array], axis=1)

    result = analyse(halves, listed(observed_entry_index), listed(obs_value), listed(obs_weight))
    result = spread(result, rows)
    return result.reshape(result.shape[0], variables, levels, rows, cols // sources)


def solution(mesh):
    placed = (
        P("mem", None, None, "row", "col"),
        P(),
        P(),
        P(),
        P(),
        P(None, "row", ("col", "mem")),
        P(None, "row", ("col", "mem")),
        P(None, "row", ("col", "mem")),
    )
    return jax.shard_map(
        body,
        mesh=mesh,
        in_specs=placed,
        out_specs=P(None, None, None, "row", ("col", "mem")),
        check_vma=False,
    )
```

```python
import jax
import jax.numpy as jnp
from jax import lax
from jax.experimental import pallas as pl
from jax.experimental.pallas import tpu as pltpu
from jax.sharding import PartitionSpec as P

STEPS = 2
PARTS = 2
ORDER = ((0, 0), (1, 0), (0, 1), (1, 1), (0, 2), (0, 3), (1, 2), (1, 3))


def pack(value, place, lane, sides):
    west, east = sides
    here = lane == place
    return (
        jnp.where(here, pltpu.roll(value, place, 1), west),
        jnp.where(here, pltpu.roll(value, place + 1, 1), east),
    )


def borders_kernel(x_ref, north_ref, south_ref, west_ref, east_ref):
    _, variables, levels, rows, cols = x_ref.shape
    lane = lax.broadcasted_iota(jnp.int32, (rows, cols), 1)

    def level(l, sides):
        for v in range(variables):
            value, place = x_ref[0, v, l], v * levels + l
            north_ref[0, pl.ds(place, 1), :] = value[:1]
            south_ref[0, pl.ds(place, 1), :] = value[rows - 1 :]
            sides = pack(value, place, lane, sides)
        return sides

    zero = jnp.zeros((rows, cols), jnp.float32)
    west_ref[0], east_ref[0] = lax.fori_loop(0, levels, level, (zero, zero), unroll=8)


def advance_kernel(final, paired, level_ref, mix_ref, *refs):
    x_ref, refs = refs[0], refs[1:]
    base_ref = None
    if paired:
        base_ref, refs = refs[0], refs[1:]
    north_ref, south_ref, west_ref, east_ref, out_ref = refs[:5]
    refs = refs[5:]
    _, variables, levels, rows, cols = x_ref.shape
    lane = lax.broadcasted_iota(jnp.int32, (rows, cols), 1)
    row = lax.broadcasted_iota(jnp.int32, (rows, cols), 0)
    west_halo, east_halo = west_ref[0], east_ref[0]

    def level(l, carry):
        values = [x_ref[0, v, l] for v in range(variables)]
        north_c, south_c, west_c, east_c, centre_c = [level_ref[i, l] for i in range(5)]
        for v in range(variables):
            value, place = values[v], v * levels + l
            north = jnp.where(row == 0, north_ref[0, pl.ds(place, 1), :], pltpu.roll(value, 1, 0))
            south = jnp.where(
                row == rows - 1, south_ref[0, pl.ds(place, 1), :], pltpu.roll(value, rows - 1, 0)
            )
            west = jnp.where(lane == 0, pltpu.roll(west_halo, cols - place, 1), pltpu.roll(value, 1, 1))
            east = jnp.where(
                lane == cols - 1, pltpu.roll(east_halo, cols - 1 - place, 1), pltpu.roll(value, cols - 1, 1)
            )
            change = north_c * north + south_c * south + west_c * west + east_c * east
            change = change + (centre_c + mix_ref[v, v]) * value
            for w in range(variables):
                if w != v:
                    change = change + mix_ref[v, w] * values[w]
            result = value + change
            if paired:
                result = 0.5 * (base_ref[0, v, l] + result)
            if final:
                scratch = refs[0]
                scratch[pl.ds(pl.multiple_of(place * rows, rows), rows), :] = result
            else:
                out_ref[0, v, l] = result
        return carry

    lax.fori_loop(0, levels, level, 0, unroll=8)
    if not final:
        borders_kernel(out_ref, *refs)
        return
    groups, width = out_ref.shape[0], out_ref.shape[3]
    for r in range(rows):
        turned = refs[0][pl.ds(r, variables * levels, stride=rows), :].T
        for g in range(groups):
            out_ref[g, 0, r] = turned[g * width : (g + 1) * width]


def edge_specs(shape):
    members, variables, levels, rows, cols = shape
    line = (members, variables * levels, cols)
    side = (members, rows, cols)
    shapes = [jax.ShapeDtypeStruct(d, jnp.float32) for d in (line, line, side, side)]
    specs = [pl.BlockSpec((1,) + d.shape[1:], lambda i: (i, 0, 0)) for d in shapes]
    return shapes, specs


def member_spec(x, start):
    return pl.BlockSpec((1,) + x.shape[1:], lambda i: (i + start, 0, 0, 0, 0))


def borders(state, part):
    x, start = state
    shapes, specs = edge_specs((part,) + x.shape[1:])
    return pl.pallas_call(
        borders_kernel,
        grid=(part,),
        in_specs=[member_spec(x, start)],
        out_specs=specs,
        out_shape=shapes,
        cost_estimate=pl.CostEstimate(flops=x.size, bytes_accessed=x.size * 4, transcendentals=0),
    )(x)


def exchanged(edges):
    north, south, west, east = edges

    def shifted(value, axis, step):
        count = lax.axis_size(axis)
        pairs = [(i, i + 1) for i in range(count - 1)]
        return lax.ppermute(value, axis, pairs if step > 0 else [(j, i) for i, j in pairs])

    return [
        shifted(south, "row", 1),
        shifted(north, "row", -1),
        shifted(east, "col", 1),
        shifted(west, "col", -1),
    ]


def advance(state, base, halos, by_level, mix, final):
    members, (_, variables, levels, rows, cols) = halos[0].shape[0], state[0].shape
    shape = (members, variables, levels, rows, cols)
    size = members * variables * levels * rows * cols
    shapes, specs = edge_specs(shape)
    scalars = pl.BlockSpec(memory_space=pltpu.SMEM)
    fields = [state] if base is None else [state, base]
    scratch = []
    if final:
        groups = lax.axis_size("mem")
        turned = (groups, members, rows, cols // groups, variables * levels)
        out_shape = [jax.ShapeDtypeStruct(turned, jnp.float32)]
        out_specs = [
            pl.BlockSpec((groups, 1) + turned[2:], lambda i: (0, i, 0, 0, 0))
        ]
        scratch = [pltpu.VMEM((variables * levels * rows, cols), jnp.float32)]
    else:
        out_shape = [jax.ShapeDtypeStruct(shape, jnp.float32)] + shapes
        out_specs = [pl.BlockSpec((1,) + shape[1:], lambda i: (i, 0, 0, 0, 0))] + specs
    out = pl.pallas_call(
        lambda *refs: advance_kernel(final, base is not None, *refs),
        grid=(members,),
        in_specs=[scalars, scalars] + [member_spec(*field) for field in fields] + specs,
        out_specs=out_specs,
        out_shape=out_shape,
        scratch_shapes=scratch,
        cost_estimate=pl.CostEstimate(flops=size * 40, bytes_accessed=size * 48, transcendentals=0),
    )(by_level, mix, *[field[0] for field in fields], *halos)
    return (out[0], 0), out[1:]


def split(value):
    high = value.astype(jnp.bfloat16)
    return high, (value - high.astype(jnp.float32)).astype(jnp.bfloat16)


def doubled(high, low, left):
    both = jnp.where(left, high.astype(jnp.float32), low.astype(jnp.float32)).astype(jnp.bfloat16)
    return jnp.concatenate([both, both], axis=1)


def stacked(high, low):
    return jnp.concatenate([high, high, low, low], axis=0)


def product(left, right):
    return lax.dot_general(left, right, (((1,), (0,)), ((), ())), preferred_element_type=jnp.float32)


def product_t(left, right):
    return lax.dot_general(left, right, (((1,), (1,)), ((), ())), preferred_element_type=jnp.float32)


def analysis_kernel(first_ref, second_ref, index_ref, root_ref, value_ref, out_ref):
    sources, part, count, entries = first_ref.shape
    members = 2 * sources * part
    halves = [ref.reshape(sources * part * count, entries) for ref in (first_ref, second_ref)]
    placed = out_ref.reshape(members * count, entries)
    cells = range(count)
    lane = lax.broadcasted_iota(jnp.int32, (members, 2 * members), 1)
    row = lax.broadcasted_iota(jnp.int32, (members, 2 * members), 0)
    left = lane < members
    left_tall = lax.broadcasted_iota(jnp.int32, (members + 16, 2 * members), 1) < members
    eye = jnp.where((lane == row) | (lane == row + members), 1.0, 0.0).astype(jnp.float32)
    means, perts, systems, gains = [], [], [], []
    for b in cells:
        x = jnp.concatenate([ref[pl.ds(b, sources * part, stride=count), :] for ref in halves], axis=0)
        mean = jnp.sum(x, axis=0, keepdims=True) * (1.0 / members)
        pert = x - mean
        index = jnp.broadcast_to(index_ref[b : b + 1], (members, entries))
        observed = jnp.take_along_axis(pert, index, axis=1)
        obs_mean = jnp.take_along_axis(jnp.broadcast_to(mean, (8, entries)), index[:8], axis=1)
        root = root_ref[b : b + 1]
        innovation = (value_ref[b : b + 1] - obs_mean) * root
        scaled = observed * root
        high, low = split(jnp.concatenate([scaled, innovation, innovation], axis=0))
        ahigh, alow = high[:members], low[:members]
        wide = jnp.concatenate(
            [jnp.concatenate([ahigh, alow], axis=1), jnp.concatenate([ahigh, alow], axis=1)], axis=0
        )
        both = product_t(doubled(high, low, left_tall), wide)
        means.append(mean)
        perts.append(pert)
        systems.append(both[:members] + (members - 1.0) * eye)
        gains.append(both[members : members + 1])
    inverses, rates = [], []
    for b in cells:
        total = 0.5 * jnp.sum(jnp.sum(systems[b] * systems[b], axis=0, keepdims=True), axis=1, keepdims=True)
        rates.append(lax.rsqrt(total))
    for b in cells:
        current = systems[b] * rates[b]
        high, low = split(current)
        square = product(doubled(high, low, left), stacked(high, low))
        shigh, slow = split(square)
        high, low = split(0.0625 * square - 0.5625 * current)
        rest = product(doubled(shigh, slow, left), stacked(high, low))
        inverses.append(2.25 * eye - 2.4375 * current + 1.6875 * square + rest)
    for b in cells:
        high, low = split(inverses[b])
        phigh, plow = split(perts[b])
        moved = product(doubled(high, low, left), stacked(phigh, plow))
        half = 0.5 * jnp.sum(inverses[b] * gains[b], axis=1, keepdims=True)
        shift = jnp.sum(moved * half, axis=0, keepdims=True) * rates[b]
        result = moved * jnp.sqrt((members - 1.0) * rates[b]) + (means[b] + shift)
        for half in range(2):
            for source in range(sources):
                start, at = (half * sources + source) * part, (2 * source + half) * part
                placed[pl.ds(at * count + b, part, stride=count), :] = result[start : start + part]


def analyse(halves, index, value, weight):
    sources, part, cells, entries = halves[0].shape
    members = 2 * sources * part
    count = 8
    small = pl.BlockSpec((count, index.shape[1]), lambda i: (i, 0))
    large = pl.BlockSpec((members, count, entries), lambda i: (0, i, 0))
    half = pl.BlockSpec((sources, part, count, entries), lambda i: (0, 0, i, 0))
    return pl.pallas_call(
        analysis_kernel,
        grid=(cells // count,),
        in_specs=[half, half, small, small, small],
        out_specs=large,
        out_shape=jax.ShapeDtypeStruct((members, cells, entries), jnp.float32),
    )(*halves, index, jnp.sqrt(weight), value)


def spread_kernel(x_ref, out_ref):
    _, cells, entries = x_ref.shape
    rows = out_ref.shape[1] // entries
    width = cells // rows
    placed = out_ref.at[0]
    for r in range(rows):
        placed[pl.ds(r, entries, stride=rows), :] = x_ref[0, r * width : (r + 1) * width, :].T


def spread(x, rows):
    members, cells, entries = x.shape
    shape = (members, entries * rows, cells // rows)
    return pl.pallas_call(
        spread_kernel,
        grid=(members,),
        in_specs=[pl.BlockSpec((1, cells, entries), lambda i: (i, 0, 0))],
        out_specs=pl.BlockSpec((1,) + shape[1:], lambda i: (i, 0, 0)),
        out_shape=jax.ShapeDtypeStruct(shape, jnp.float32),
    )(x)


def body(
    background_sample,
    coupling,
    diffusion,
    wind_row,
    wind_col,
    observed_entry_index,
    obs_value,
    obs_weight,
):
    members, variables, levels, rows, cols = background_sample.shape
    by_level = jnp.stack(
        [
            diffusion + 0.5 * wind_row,
            diffusion - 0.5 * wind_row,
            diffusion + 0.5 * wind_col,
            diffusion - 0.5 * wind_col,
            -4.0 * diffusion,
        ]
    )
    part = members // PARTS
    states = [(background_sample, i * part) for i in range(PARTS)]
    edges = [borders(state, part) for state in states]
    halos = [exchanged(edge) for edge in edges]
    middles = [None] * PARTS
    gate = None
    for i, turn in ORDER:
        table = by_level if gate is None else lax.optimization_barrier((by_level, gate))[0]
        if turn % 2 == 0:
            middles[i], edge = advance(states[i], None, halos[i], table, coupling, False)
        else:
            last = turn == 2 * STEPS - 1
            states[i], edge = advance(middles[i], states[i], halos[i], table, coupling, last)
        if edge:
            gate, halos[i] = edge[2], exchanged(edge)
        else:
            gate = states[i][0][:1, :1, :1, :1, :1]
    sources = lax.axis_size("mem")
    cells = rows * (cols // sources)
    halves = [
        lax.all_to_all(state, "mem", split_axis=0, concat_axis=0).reshape(
            sources, part, cells, variables * levels
        )
        for state, _ in states
    ]

    def listed(array):
        array = array.reshape(array.shape[0], cells).T
        return jnp.concatenate([array, array], axis=1)

    result = analyse(halves, listed(observed_entry_index), listed(obs_value), listed(obs_weight))
    result = spread(result, rows)
    return result.reshape(result.shape[0], variables, levels, rows, cols // sources)


def solution(mesh):
    placed = (
        P("mem", None, None, "row", "col"),
        P(),
        P(),
        P(),
        P(),
        P(None, "row", ("col", "mem")),
        P(None, "row", ("col", "mem")),
        P(None, "row", ("col", "mem")),
    )
    return jax.shard_map(
        body,
        mesh=mesh,
        in_specs=placed,
        out_specs=P(None, None, None, "row", ("col", "mem")),
        check_vma=False,
    )
```
